32 devices in a mesh: walk: 4 (over y, x), chol: 8 (over z, core).
Axes of the slice: x: 2, y: 2, z: 4, core: 2. Of those that a mesh axis runs over, the one named last changes fastest.
Arguments:
- orbitals: bfloat16 [256, 64, 1024], P(('walk', 'chol')), may hold values from -6 to 6
- cholesky: bfloat16 [96, 64, 1024], P('chol'), may hold values from -0.1875 to 0.1875
- parents: int32 [256], P(('walk', 'chol')), may hold values from 0 to 255, as said below
- counts: int32 [4, 8], P('walk', 'chol'), may hold values from 1 to 8, as said below
- steps: bfloat16 [256, 64, 1024], P(('walk', 'chol')), may hold values from -6 to 6
Outputs:
- energy: float32 [256], P(('walk', 'chol'))
- parent_grad: float32 [256, 64, 1024], P(('walk', 'chol'))
The draws below stay inside these ranges and needn't reach their ends.
Inputs may be any that keep to these rules, and one draw needn't show every extreme that they name: The parent of a new walker lies on the same index of chol as the walker. Of one device's new walkers at most 2 have parents on any one index of walk, and on some index exactly 2. The first counts entries of a device's 8 new walkers are live; in every draw some device is full.
All inputs are finite; a program needn't handle non-finite values.
Results may differ from the reference program's by a relative error of at most 0.0044.
Values may be sent and summed in bfloat16 or wider, within the bound.
No kernel may reach another device: no remote copies, remote signals or barrier semaphores. Data moves between devices by JAX's collectives and lax.ppermute only.
A program may use at most 128 MiB of HBM per device.

```python
import jax
import jax.numpy as jnp
from jax import lax

BASIS = 1024
ELECTRONS = 64
WALK_DEV = 8
CHOL_DEV = 12
WALKERS = 256
VECTORS = 96
N_WALK = 4
N_CHOL = 8


def draw_parents(key, part):
    devices_all = N_WALK * N_CHOL
    first, second, third, fourth = jax.random.split(jax.random.fold_in(key, 11), 4)
    walk_orders = jax.vmap(lambda sub: jax.random.permutation(sub, N_WALK))(jax.random.split(first, devices_all))
    allow = 1 if WALK_DEV // 2 < N_WALK else 0
    offset = jax.random.randint(second, (devices_all, 1), 0, 2) * allow
    within = jnp.arange(WALK_DEV, dtype=jnp.int32)[None, :]
    choice_index = jnp.where(within < 2, 0, (within + offset) // 2)
    shuffles = jax.vmap(lambda sub: jax.random.permutation(sub, WALK_DEV))(jax.random.split(third, devices_all))
    choice_index = jnp.take_along_axis(choice_index, shuffles, axis=1)
    source_walk = jnp.take_along_axis(walk_orders, choice_index, axis=1)
    source_slot = jax.random.randint(fourth, (devices_all, WALK_DEV), 0, WALK_DEV)
    chol_index = (jnp.arange(devices_all, dtype=jnp.int32) % N_CHOL)[:, None]
    parent_ids = (source_walk * N_CHOL + chol_index) * WALK_DEV + source_slot
    return parent_ids.reshape(-1).astype(jnp.int32)


def draw_counts(key, part):
    first, second = jax.random.split(jax.random.fold_in(key, 23), 2)
    lowered = jax.random.randint(first, (N_WALK * N_CHOL,), 0, WALK_DEV)
    lowered = lowered * jax.random.randint(second, (N_WALK * N_CHOL,), 0, 2)
    filled = jnp.maximum(WALK_DEV - lowered, 1)
    pick = jax.random.randint(jax.random.fold_in(key, 29), (), 0, N_WALK * N_CHOL)
    filled = jnp.where(jnp.arange(N_WALK * N_CHOL) == pick, WALK_DEV, filled)
    return filled.reshape(N_WALK, N_CHOL).astype(jnp.int32)


def block_levels(own_key, extent, cuts, smallest, high):
    factor_of, own = 1.0, jax.random.fold_in(own_key, 6)
    for dim, blocks in cuts:
        steps = jnp.exp(jax.random.uniform(jax.random.fold_in(own, dim), (blocks,), jnp.float32, smallest / len(cuts), high / len(cuts)))
        factor_of = factor_of * jnp.repeat(steps, extent[dim] // blocks).reshape([-1 if axis == dim else 1 for axis in range(len(extent))])
    return factor_of


def normal_values(key, extent, width, most, cuts=(), held_as=jnp.bfloat16):
    values = width * jax.random.normal(key, extent, jnp.float32)
    if cuts:
        values = values * block_levels(key, extent, cuts, -0.22, 0.18)
    return jnp.clip(values, -most, most).astype(held_as)


def setup_inputs(seed: int = 0) -> dict:
    splits = jax.random.split(jax.random.key(seed), 6)
    orbitals = normal_values(splits[0], (WALKERS, ELECTRONS, BASIS), 1.0, 6.0, ((0, 32),))
    cholesky = normal_values(splits[1], (VECTORS, ELECTRONS, BASIS), BASIS ** -0.5, 0.1875, ((0, 8),))
    parents = draw_parents(jax.random.fold_in(splits[5], 71), 0)
    counts = draw_counts(jax.random.fold_in(splits[5], 71), 0)
    steps = normal_values(splits[4], (WALKERS, ELECTRONS, BASIS), 1.0, 6.0, ((0, 32),))
    return dict(orbitals=orbitals, cholesky=cholesky, parents=parents, counts=counts, steps=steps)


def reference(orbitals, cholesky, parents, counts, steps):
    clones = (orbitals[parents].astype(jnp.float32) + steps.astype(jnp.float32)).astype(jnp.bfloat16)
    position = jnp.arange(WALKERS, dtype=jnp.int32)
    flat_counts = counts.reshape(-1)
    alive = (position % WALK_DEV < flat_counts[position // WALK_DEV]).astype(jnp.float32)
    blocks = clones.reshape(N_WALK, WALK_DEV * N_CHOL, ELECTRONS, BASIS)

    def shard_step(total, shard):
        vectors = lax.dynamic_slice_in_dim(cholesky, (shard * CHOL_DEV).astype(jnp.int32), CHOL_DEV, 0).astype(jnp.float32)

        def one_block(walkers):
            walk_f = walkers.astype(jnp.float32)
            intersection = jnp.einsum("gip,wjp->wgij", vectors, walk_f).astype(jnp.bfloat16).astype(jnp.float32)
            part = -jnp.einsum("wgji,gip->wjp", intersection, vectors)
            part = lax.optimization_barrier(part.astype(jnp.bfloat16))
            return part.astype(jnp.float32)

        parts = lax.map(one_block, blocks).reshape(WALKERS, ELECTRONS, BASIS)
        return total + parts, None

    start = jnp.zeros((WALKERS, ELECTRONS, BASIS), jnp.float32)
    summed, _ = lax.scan(shard_step, start, jnp.arange(N_CHOL, dtype=jnp.int32))
    gradient = summed * alive[:, None, None]
    energy = 0.5 * jnp.sum(clones.astype(jnp.float32) * gradient, axis=(1, 2))
    parent_grad = jax.ops.segment_sum(gradient, parents, num_segments=WALKERS)
    return energy, parent_grad
```

```python
import functools

import jax
import jax.numpy as jnp
from jax import lax
from jax.experimental import pallas as pl
from jax.experimental.pallas import tpu as pltpu
from jax.sharding import PartitionSpec as P

CAP = 2
AXES = ("walk", "chol")
VMEM = pl.BlockSpec(memory_space=pltpu.VMEM)
SMEM = pl.BlockSpec(memory_space=pltpu.SMEM)
META_ROWS = 16


def params(mib):
    return pltpu.CompilerParams(vmem_limit_bytes=mib * 1024 * 1024)


def pack_kernel(walks, chols, parents_ref, counts_ref, steps_ref, *outs):
    per_device, electrons, _ = steps_ref.shape
    me = lax.axis_index("walk")
    group = [parents_ref[j] // (chols * per_device) for j in range(per_device)]
    slot = [lax.rem(parents_ref[j], per_device) for j in range(per_device)]
    alive = [(j < counts_ref[0, 0]).astype(jnp.int32) for j in range(per_device)]
    rank = []
    for j in range(per_device):
        r = jnp.int32(0)
        for i in range(j):
            r = r + (group[i] == group[j]).astype(jnp.int32)
        rank.append(jnp.minimum(r, CAP - 1))
    rows = lax.broadcasted_iota(jnp.int32, (META_ROWS, outs[0].shape[1]), 0)
    for m in range(walks):
        out = outs[m]
        if walks * CAP > per_device:
            out[...] = jnp.zeros_like(out)
        meta = jnp.zeros(rows.shape, jnp.float32)
        for r in range(CAP):
            at = jnp.int32(0)
            live = jnp.int32(0)
            for j in range(per_device):
                hit = ((lax.bitwise_xor(group[j], me) == m) & (rank[j] == r)).astype(jnp.int32)
                at = at + hit * slot[j]
                live = live + hit * alive[j]
            meta = jnp.where(rows == r, at.astype(jnp.float32), meta)
            meta = jnp.where(rows == CAP + r, live.astype(jnp.float32), meta)
        out[CAP * electrons :, :] = meta.astype(out.dtype)
        for j in range(per_device):
            for r in range(CAP):

                @pl.when((lax.bitwise_xor(group[j], me) == m) & (rank[j] == r))
                def _(j=j, r=r, out=out):
                    out[r * electrons : (r + 1) * electrons, :] = steps_ref[j]


def clone_kernel(walks, orbitals_ref, *refs):
    got, clones, meta_out = refs[:walks], refs[walks], refs[walks + 1]
    _, electrons, _ = orbitals_ref.shape
    for m in range(walks):
        meta = got[m][CAP * electrons :, 0:128].astype(jnp.float32)
        for r in range(CAP):
            s = m * CAP + r
            at = jnp.max(meta[r : r + 1, :]).astype(jnp.int32)
            live = jnp.max(meta[CAP + r : CAP + r + 1, :]).astype(jnp.int32)
            meta_out[s] = at
            meta_out[walks * CAP + s] = live
            step = got[m][r * electrons : (r + 1) * electrons, :]
            clone = orbitals_ref[at].astype(jnp.float32) + step.astype(jnp.float32)
            clones[s * electrons : (s + 1) * electrons, :] = clone.astype(clones.dtype)


def exchange_kernel(counts, electrons, first, *refs):
    n = len(counts)
    clones, vectors = refs[0], refs[1 : 1 + n]
    acc_in = None if first else refs[1 + n]
    acc = refs[-1]
    rows = clones.shape[0]
    order = [(k, i) for k in range(n) for i in range(counts[k])]
    lane = lax.broadcasted_iota(jnp.int32, (electrons, 2 * electrons), 1) < electrons
    started = not first
    for at in range(0, len(order), 4):
        group = order[at : at + 4]
        block = [vectors[k][i] for k, i in group]
        left = jnp.concatenate(block, axis=0) if len(block) > 1 else block[0]
        inter = lax.dot_general(
            left, clones[...], (((1,), (1,)), ((), ())), preferred_element_type=jnp.float32
        )
        columns = []
        for pair in range(0, len(block), 2):
            top = inter[pair * electrons : (pair + 1) * electrons, :]
            full = pair + 1 < len(block)
            bottom = inter[(pair + 1) * electrons : (pair + 2) * electrons, :] if full else None
            parts = []
            for w in range(0, rows // electrons, 2):
                a = top[:, w * electrons : (w + 2) * electrons]
                ra = pltpu.roll(a, electrons, 1)
                if full:
                    b = bottom[:, w * electrons : (w + 2) * electrons]
                    rb = pltpu.roll(b, electrons, 1)
                    parts += [jnp.where(lane, a, rb), jnp.where(lane, ra, b)]
                else:
                    parts += [jnp.where(lane, a, 0.0), jnp.where(lane, ra, 0.0)]
            columns.append(jnp.concatenate([x.astype(jnp.bfloat16) for x in parts], axis=0))
        if len(block) % 2:
            left = jnp.concatenate([left, jnp.zeros_like(block[0])], axis=0)
        right = jnp.concatenate(columns, axis=1) if len(columns) > 1 else columns[0]
        term = jnp.dot(right, left, preferred_element_type=jnp.float32)
        if started:
            source = acc if at else acc_in
            acc[...] = source[...] + term
        else:
            acc[...] = term
            started = True


def exchange(clones, pieces, acc):
    rows, basis = clones.shape
    electrons = pieces[0].shape[1]
    counts = [p.shape[0] for p in pieces]
    total = sum(counts)
    args = [clones, *pieces] + ([] if acc is None else [acc])
    return pl.pallas_call(
        functools.partial(exchange_kernel, counts, electrons, acc is None),
        out_shape=jax.ShapeDtypeStruct((rows, basis), jnp.float32),
        in_specs=[VMEM] * len(args),
        out_specs=VMEM,
        input_output_aliases={} if acc is None else {len(args) - 1: 0},
        compiler_params=params(24),
        cost_estimate=pl.CostEstimate(
            flops=4 * rows * total * electrons * basis,
            bytes_accessed=total * electrons * basis * 2,
            transcendentals=0,
        ),
    )(*args)


def round_kernel(acc, out):
    out[...] = acc[...].astype(out.dtype)


def finish_kernel(walks, per_device, acc, other, clones, meta, grad, *energies):
    slots = walks * CAP
    electrons = clones.shape[0] // slots
    grad[...] = jnp.zeros_like(grad)
    for s in range(slots):
        span = pl.ds(s * electrons, electrons)
        live = meta[slots + s].astype(jnp.float32)
        g = (acc[span, :] + other[span, :].astype(jnp.float32)) * (-live)
        e = 0.5 * jnp.sum(clones[span, :].astype(jnp.float32) * g)
        energies[s // CAP][s % CAP] = jnp.full(energies[0].shape[1:], e, jnp.float32)
        at = jnp.clip(meta[s], 0, per_device - 1)
        grad[at] = grad[at] + g


def body(orbitals, cholesky, parents, counts, steps):
    walks = lax.axis_size("walk")
    chols = lax.axis_size("chol")
    per_device, electrons, basis = orbitals.shape
    n = cholesky.shape[0]
    levels = chols // 2
    slots = walks * CAP
    w = lax.axis_index("walk")

    def send(x, move):
        pairs = []
        for a in range(walks):
            for z in range(levels):
                for k in range(2):
                    b, y, i = move(a, z, k)
                    pairs.append((a * chols + z * 2 + k, b * chols + y * 2 + i))
        return lax.ppermute(x, AXES, pairs)

    def along(x, t):
        return send(x, lambda a, z, k: (a, (z + t) % levels, k))

    def across(x, m):
        return send(x, lambda a, z, k: (a ^ m, z, k))

    def swap(x):
        return send(x, lambda a, z, k: (a, z, 1 - k))

    parity = jnp.int32(0)
    for bit in range(walks.bit_length()):
        parity = parity ^ ((w >> bit) & 1)

    def plan(share):
        a = min(share, n // walks)
        while a and (n - a * walks) % 4:
            a -= 1
        return a, (n - a * walks) // 4

    def piece(a, e):
        parts = []
        if e:
            parts.append(lax.dynamic_slice_in_dim(cholesky, walks * a + parity * 2 * e, e, 0))
        if a:
            parts.append(lax.dynamic_slice_in_dim(cholesky, w * a, a, 0))
        if e:
            parts.append(lax.dynamic_slice_in_dim(cholesky, walks * a + parity * 2 * e + e, e, 0))
        return jnp.concatenate(parts, axis=0) if len(parts) > 1 else parts[0]

    up, down = plan(n // (3 * walks)), plan(n // walks)
    n_up = levels // 2
    arrived = []
    near = along(piece(*down), -1)
    far = along(piece(*up), 1)
    arrived.append((near, down))
    arrived.append((far, up))
    for t in range(2, max(n_up, levels - 1 - n_up) + 1):
        if t <= levels - 1 - n_up:
            near = along(near, -1)
            arrived.append((near, down))
        if t <= n_up:
            far = along(far, 1)
            arrived.append((far, up))

    packed = pl.pallas_call(
        functools.partial(pack_kernel, walks, chols),
        out_shape=[jax.ShapeDtypeStruct((CAP * electrons + META_ROWS, basis), steps.dtype)] * walks,
        in_specs=[SMEM, SMEM, VMEM],
        out_specs=[VMEM] * walks,
        compiler_params=params(16),
    )(parents, counts, steps)
    got = [packed[0]] + [across(packed[m], m) for m in range(1, walks)]
    clones, meta = pl.pallas_call(
        functools.partial(clone_kernel, walks),
        out_shape=[
            jax.ShapeDtypeStruct((slots * electrons, basis), jnp.bfloat16),
            jax.ShapeDtypeStruct((2 * slots,), jnp.int32),
        ],
        in_specs=[VMEM] * (1 + walks),
        out_specs=[VMEM, SMEM],
        compiler_params=params(16),
    )(orbitals, *got)
    partner = swap(clones)

    mine, theirs = None, None
    pending = [cholesky]
    for x, (a, e) in arrived:
        pending = pending + [x]
        mine, theirs = exchange(clones, pending, mine), exchange(partner, pending, theirs)
        pending = []
        for m in range(1, walks):
            part = x[: e + a] if m == 1 else x[e:] if m == 2 else x[e : e + a]
            if part.shape[0]:
                pending.append(across(part, m))
    theirs = exchange(partner, pending, theirs)
    rounded = pl.pallas_call(
        round_kernel,
        out_shape=jax.ShapeDtypeStruct(theirs.shape, jnp.bfloat16),
        in_specs=[VMEM],
        out_specs=VMEM,
        compiler_params=params(16),
    )(theirs)
    other = swap(rounded)
    mine = exchange(clones, pending, mine)
    grad, *energies = pl.pallas_call(
        functools.partial(finish_kernel, walks, per_device),
        out_shape=[jax.ShapeDtypeStruct((per_device, electrons, basis), jnp.float32)]
        + [jax.ShapeDtypeStruct((CAP, 8, 128), jnp.float32)] * walks,
        in_specs=[VMEM, VMEM, VMEM, SMEM],
        out_specs=[VMEM] * (1 + walks),
        compiler_params=params(24),
    )(mine, other, clones, meta)
    back = [energies[0]] + [across(energies[m], m) for m in range(1, walks)]
    table = jnp.concatenate([b[:, 0, 0] for b in back])
    source = (parents // (chols * per_device)) ^ w
    position = jnp.arange(per_device, dtype=jnp.int32)
    earlier = (source[:, None] == source[None, :]) & (position[None, :] < position[:, None])
    rank = jnp.sum(earlier.astype(jnp.int32), axis=1)
    pick = (source * CAP + rank)[:, None] == jnp.arange(slots, dtype=jnp.int32)[None, :]
    energy = jnp.sum(jnp.where(pick, table[None, :], 0.0), axis=1)
    return energy, grad


def solution(mesh):
    placed = (
        P(("walk", "chol"), None, None),
        P("chol", None, None),
        P(("walk", "chol")),
        P("walk", "chol"),
        P(("walk", "chol"), None, None),
    )
    return jax.shard_map(
        body,
        mesh=mesh,
        in_specs=placed,
        out_specs=(P(("walk", "chol")), P(("walk", "chol"), None, None)),
        check_vma=False,
    )
```
